32 devices in a mesh: tile: 8 (over y, x, core), aux: 4 (over z).
Axes of the slice: x: 2, y: 2, z: 4, core: 2. Of those that a mesh axis runs over, the one named last changes fastest.
Arguments:
- amps: bfloat16 [8, 8, 128, 128], P('tile'), may hold values from -6 to 6
- fitted: bfloat16 [2048, 8, 128], P('aux'), may hold values from -0.375 to 0.375
- screen: int32 [16, 8], P('aux'), may hold values 0 or 1
- owner: int32 [8], replicated, may hold values from 0 to 7, each once
- eps_occ: float32 [8], replicated, may hold values from -2 to -0.5
- eps_vir: float32 [128], replicated, may hold values from 0.5 to 2
Outputs:
- update: bfloat16 [8, 128, 8, 128], P(None, None, 'tile')
The draws below stay inside these ranges and needn't reach their ends.
Inputs may be any that keep to these rules, and one draw needn't show every extreme that they name: owner is a permutation of the occupied orbitals.
All inputs are finite; a program needn't handle non-finite values. No bound on the sum of `screen` on one device may be relied on, other than what follows from the above.
Results may differ from the reference program's by a relative error of at most 0.0034.
Values may be sent and summed in bfloat16 or wider, within the bound.
No kernel may reach another device: no remote copies, remote signals or barrier semaphores. Data moves between devices by JAX's collectives and lax.ppermute only.
A program may use at most 64 MiB of HBM per device.

```python
import jax
import jax.numpy as jnp

V = 128
QBLK = 128
O = 8
NAUX = 2048


def place_ends(entries, stream_key, least, top_value):
    spot = [jax.random.randint(jax.random.fold_in(stream_key, axis), (), 0, length) for axis, length in enumerate(entries.shape)]
    main_axis = entries.shape.index(max(entries.shape))
    beside = spot[:main_axis] + [(spot[main_axis] + 1) % entries.shape[main_axis]] + spot[main_axis + 1:]
    return entries.at[tuple(spot)].set(least).at[tuple(beside)].set(top_value)


def steps_of(own_key, extent, cuts, smallest, high):
    def one(axis_at, shards_of):
        steps = jax.random.uniform(jax.random.fold_in(jax.random.fold_in(own_key, 6), axis_at), (shards_of,), jnp.float32, smallest / len(cuts), high / len(cuts))
        return jnp.repeat(jnp.exp(steps), extent[axis_at] // shards_of).reshape((-1,) + (1,) * (len(extent) - axis_at - 1))

    loudness = one(*cuts[0])
    for cut in cuts[1:]:
        loudness = loudness * one(*cut)
    return loudness


def noise(stream_key, dims, width, reach, cuts=(), dtype=jnp.bfloat16):
    result = width * jax.random.normal(stream_key, dims, jnp.float32)
    if cuts:
        result = result * steps_of(stream_key, dims, cuts, -0.22, 0.18)
    return jnp.clip(result, -reach, reach).astype(dtype)


def setup_inputs(seed: int = 0) -> dict:
    seeds = jax.random.split(jax.random.key(seed), 7)
    amps = noise(seeds[0], (O, O, V, V), 1.0, 6.0, ((0, 8),))
    fitted = noise(seeds[1], (NAUX, O, V), ((NAUX * O * V) ** -0.25), 0.375, ((0, 4),))
    screen = place_ends((jax.random.randint(seeds[2], (NAUX // QBLK, O), 0, 4) < 3).astype(jnp.int32), jax.random.fold_in(seeds[2], 1), 0, 1)
    owner = jax.random.permutation(seeds[3], O).astype(jnp.int32)
    eps_occ = jnp.clip(jax.random.uniform(seeds[4], (O,), jnp.float32, -2.0, -0.5), -2.0, -0.5)
    eps_vir = jnp.clip(jax.random.uniform(seeds[5], (V,), jnp.float32, 0.5, 2.0), 0.5, 2.0)
    return dict(amps=amps, fitted=fitted, screen=screen, owner=owner, eps_occ=eps_occ, eps_vir=eps_vir)


def reference(amps, fitted, screen, owner, eps_occ, eps_vir):
    tile_mask = jnp.repeat(screen, QBLK, axis=0).astype(jnp.bfloat16)
    screened = fitted * tile_mask[:, :, None]
    permuted = amps[:, owner].astype(jnp.float32)
    intermed = jnp.einsum("qkc,kpcb->qpb", screened.astype(jnp.float32), permuted).astype(jnp.bfloat16)
    cycle_term = jnp.einsum("qia,qpb->iapb", screened.astype(jnp.float32), intermed.astype(jnp.float32))
    denominator = eps_vir[None, :, None, None] + eps_vir[None, None, None, :] - eps_occ[:, None, None, None] - eps_occ[owner][None, None, :, None]
    return (cycle_term / denominator).astype(jnp.bfloat16)
```

```python
import functools

import jax
import jax.numpy as jnp
from jax import lax
from jax.experimental import pallas as pl
from jax.experimental.pallas import tpu as pltpu
from jax.sharding import PartitionSpec as P


def hop_to(i, k, n):
    return i ^ k if n & (n - 1) == 0 else (i + k) % n


def hop_from(i, k, n):
    return i ^ k if n & (n - 1) == 0 else (i + n - k) % n


def pack_kernel(groups, owner_ref, own_ref, mate_ref, *out_refs):
    me = lax.axis_index("tile")
    for step, out_ref in enumerate(out_refs):
        slot = 2 * hop_to(me // 2, step, groups) + me % 2
        column = owner_ref[slot]
        out_ref[0] = own_ref[column]
        out_ref[1] = mate_ref[column]


def cycle_kernel(groups, aux_count, share_rows, screened_ref, flipped_ref, *refs):
    piece_refs, out_refs, amps_ref = refs[:groups], refs[groups:-1], refs[-1]
    me = lax.axis_index("tile")
    virt = amps_ref.shape[1]
    for step, piece_ref in enumerate(piece_refs):
        group = hop_from(me // 2, step, groups)
        for part in range(2):
            k = 2 * group + (me + part) % 2
            amps_ref[pl.ds(pl.multiple_of(k * virt, virt), virt), :] = piece_ref[part]
    inter = jnp.dot(
        screened_ref[...], amps_ref[...], preferred_element_type=jnp.float32
    ).astype(jnp.bfloat16)
    block = share_rows * virt
    for step, out_ref in enumerate(out_refs):
        share = hop_to(lax.axis_index("aux"), step, aux_count)
        rows = flipped_ref[pl.ds(pl.multiple_of(share * block, block), block), :]
        partial = jnp.dot(rows, inter, preferred_element_type=jnp.float32)
        out_ref[...] = partial.reshape(out_ref.shape).astype(out_ref.dtype)


def join_kernel(aux_count, share_rows, *refs):
    piece_refs, out_ref = refs[:-1], refs[-1]
    me = lax.axis_index("aux")
    for step, piece_ref in enumerate(piece_refs):
        share = hop_from(me, step, aux_count)
        out_ref[pl.ds(share * share_rows, share_rows)] = piece_ref[...]


VMEM = pl.BlockSpec(memory_space=pltpu.VMEM)
SMEM = pl.BlockSpec(memory_space=pltpu.SMEM)


def room(bytes_used):
    return pltpu.CompilerParams(vmem_limit_bytes=bytes_used + (1 << 20))


def on_device(amps, fitted, screen, owner, eps_occ, eps_vir):
    virt = amps.shape[-1]
    aux_here, occ_rows, _ = fitted.shape
    tile_count, aux_count = lax.axis_size("tile"), lax.axis_size("aux")
    groups = tile_count // 2
    share_rows = -(-occ_rows // aux_count)
    padded_rows = share_rows * aux_count

    own = amps[0]
    mate = lax.ppermute(own, "tile", [(t, t ^ 1) for t in range(tile_count)])
    tile_piece = jax.ShapeDtypeStruct((2, virt, virt), amps.dtype)
    packed = pl.pallas_call(
        functools.partial(pack_kernel, groups),
        out_shape=[tile_piece] * groups,
        in_specs=[SMEM, VMEM, VMEM],
        out_specs=[VMEM] * groups,
        compiler_params=room(6 * own.size),
    )(owner, own, mate)
    pieces = [packed[0]] + [
        lax.ppermute(
            packed[step],
            "tile",
            [(t, 2 * hop_to(t // 2, step, groups) + t % 2) for t in range(tile_count)],
        )
        for step in range(1, groups)
    ]

    tile_mask = jnp.repeat(screen, aux_here // screen.shape[0], axis=0).astype(fitted.dtype)
    screened = fitted * tile_mask[:, :, None]
    flat = screened.reshape(aux_here, occ_rows * virt)
    flipped = jnp.pad(
        screened.transpose(1, 2, 0).reshape(occ_rows * virt, aux_here),
        ((0, (padded_rows - occ_rows) * virt), (0, 0)),
    )
    share = (share_rows, virt, virt)
    partials = pl.pallas_call(
        functools.partial(cycle_kernel, groups, aux_count, share_rows),
        out_shape=[jax.ShapeDtypeStruct(share, jnp.float32)]
        + [jax.ShapeDtypeStruct(share, jnp.bfloat16)] * (aux_count - 1),
        in_specs=[VMEM] * (2 + groups),
        out_specs=[VMEM] * aux_count,
        scratch_shapes=[pltpu.VMEM((occ_rows * virt, virt), amps.dtype)],
        compiler_params=room(2 * flat.size + 2 * flipped.size + 8 * own.size + 8 * padded_rows * virt * virt),
    )(flat, flipped, *pieces)

    def spread(value, step):
        perm = [(z, hop_to(z, step, aux_count)) for z in range(aux_count)]
        return lax.ppermute(value, "aux", perm)

    cycle = partials[0]
    for step in range(1, aux_count):
        cycle = cycle + spread(partials[step], step).astype(jnp.float32)

    own_owner = lax.dynamic_index_in_dim(owner, lax.axis_index("tile"), 0, keepdims=False)
    eps_slot = lax.dynamic_index_in_dim(eps_occ, own_owner, 0, keepdims=False)
    eps_share = lax.dynamic_slice_in_dim(
        jnp.pad(eps_occ, (0, padded_rows - occ_rows)),
        lax.axis_index("aux") * share_rows,
        share_rows,
        0,
    )
    virt_pair = eps_vir[None, :, None] + eps_vir[None, None, :] - eps_slot
    divided = (cycle / (virt_pair - eps_share[:, None, None])).astype(jnp.bfloat16)

    shares = [divided] + [spread(divided, step) for step in range(1, aux_count)]
    joined = pl.pallas_call(
        functools.partial(join_kernel, aux_count, share_rows),
        out_shape=jax.ShapeDtypeStruct((padded_rows, virt, virt), jnp.bfloat16),
        in_specs=[VMEM] * aux_count,
        compiler_params=room(8 * padded_rows * virt * virt),
    )(*shares)
    return joined[:occ_rows, :, None, :]


def solution(mesh):
    placed = (P("tile", None, None, None), P("aux", None, None), P("aux", None), P(), P(), P())
    return jax.shard_map(
        on_device,
        mesh=mesh,
        in_specs=placed,
        out_specs=P(None, None, "tile", None),
        check_vma=False,
    )
```

```python
import functools

import jax
import jax.numpy as jnp
from jax import lax
from jax.experimental import pallas as pl
from jax.experimental.pallas import tpu as pltpu
from jax.sharding import PartitionSpec as P


def hop_to(i, k, n):
    return i ^ k if n & (n - 1) == 0 else (i + k) % n


def hop_from(i, k, n):
    return i ^ k if n & (n - 1) == 0 else (i + n - k) % n


def pack_kernel(groups, owner_ref, own_ref, mate_ref, *out_refs):
    me = lax.axis_index("tile")
    for step, out_ref in enumerate(out_refs):
        slot = 2 * hop_to(me // 2, step, groups) + me % 2
        column = owner_ref[slot]
        out_ref[0] = own_ref[column]
        out_ref[1] = mate_ref[column]


def screen_kernel(flat_ref, screen_ref, owner_ref, eps_occ_ref, eps_vir_ref, out_ref, denominator_ref):
    blocks, occ_rows = screen_ref.shape
    share_rows, virt, _ = denominator_ref.shape
    size = flat_ref.shape[0] // blocks
    for block in range(blocks):
        for k in range(occ_rows):
            where = (pl.ds(block * size, size), pl.ds(k * virt, virt))
            tile = flat_ref[where]
            out_ref[where] = jnp.where(screen_ref[block, k] != 0, tile, jnp.zeros_like(tile))
    eps_row = jnp.broadcast_to(eps_vir_ref[...], (virt, virt))
    eps_slot = eps_occ_ref[owner_ref[lax.axis_index("tile")]]
    virt_pair = eps_row.T + eps_row - eps_slot
    for row in range(share_rows):
        i = jnp.minimum(lax.axis_index("aux") * share_rows + row, occ_rows - 1)
        denominator_ref[row] = virt_pair - eps_occ_ref[i]


def cycle_kernel(groups, aux_count, screened_ref, *refs):
    piece_refs, out_refs, amps_ref = refs[:groups], refs[groups:-1], refs[-1]
    me = lax.axis_index("tile")
    occ_rows, virt = screened_ref.shape[1] // amps_ref.shape[1], amps_ref.shape[1]
    for step, piece_ref in enumerate(piece_refs):
        group = hop_from(me // 2, step, groups)
        for part in range(2):
            k = 2 * group + (me + part) % 2
            amps_ref[pl.ds(pl.multiple_of(k * virt, virt), virt), :] = piece_ref[part]
    inter = jnp.dot(
        screened_ref[...], amps_ref[...], preferred_element_type=jnp.float32
    ).astype(jnp.bfloat16)
    share_rows = out_refs[0].shape[0]
    last = (occ_rows - share_rows) * virt
    for step, out_ref in enumerate(out_refs):
        share = hop_to(lax.axis_index("aux"), step, aux_count)
        start = jnp.minimum(share * share_rows * virt, last)
        columns = screened_ref[:, pl.ds(pl.multiple_of(start, virt), share_rows * virt)]
        flipped = lax.dot_general(
            inter, columns, (((0,), (0,)), ((), ())), preferred_element_type=jnp.float32
        )
        for row in range(share_rows):
            out_ref[row] = flipped[:, row * virt : (row + 1) * virt].T.astype(out_ref.dtype)


def join_kernel(aux_count, share_rows, *refs):
    piece_refs, out_ref = refs[:-1], refs[-1]
    me = lax.axis_index("aux")
    for step, piece_ref in enumerate(piece_refs):
        share = hop_from(me, step, aux_count)
        out_ref[pl.ds(share * share_rows, share_rows)] = piece_ref[...]


VMEM = pl.BlockSpec(memory_space=pltpu.VMEM)
SMEM = pl.BlockSpec(memory_space=pltpu.SMEM)


def room(bytes_used):
    return pltpu.CompilerParams(vmem_limit_bytes=bytes_used + (1 << 20))


def on_device(amps, fitted, screen, owner, eps_occ, eps_vir):
    virt = amps.shape[-1]
    aux_here, occ_rows, _ = fitted.shape
    tile_count, aux_count = lax.axis_size("tile"), lax.axis_size("aux")
    groups = tile_count // 2
    share_rows = -(-occ_rows // aux_count)
    padded_rows = share_rows * aux_count

    own = amps[0]
    mate = lax.ppermute(own, "tile", [(t, t ^ 1) for t in range(tile_count)])
    flat = fitted.reshape(aux_here, occ_rows * virt)
    mate, flat = lax.optimization_barrier((mate, flat))
    tile_piece = jax.ShapeDtypeStruct((2, virt, virt), amps.dtype)
    packed = pl.pallas_call(
        functools.partial(pack_kernel, groups),
        name="pack",
        out_shape=[tile_piece] * groups,
        in_specs=[SMEM, VMEM, VMEM],
        out_specs=[VMEM] * groups,
        compiler_params=room(6 * own.size),
    )(owner, own, mate)
    pieces = [packed[0]] + [
        lax.ppermute(
            packed[step],
            "tile",
            [(t, 2 * hop_to(t // 2, step, groups) + t % 2) for t in range(tile_count)],
        )
        for step in range(1, groups)
    ]

    share = (share_rows, virt, virt)
    screened, denominator = pl.pallas_call(
        screen_kernel,
        name="screen",
        out_shape=[
            jax.ShapeDtypeStruct(flat.shape, flat.dtype),
            jax.ShapeDtypeStruct(share, jnp.float32),
        ],
        in_specs=[VMEM, SMEM, SMEM, SMEM, VMEM],
        out_specs=[VMEM, VMEM],
        compiler_params=room(4 * flat.size + 4 * share_rows * virt * virt),
    )(flat, screen, owner, eps_occ, eps_vir[None, :])
    partials = pl.pallas_call(
        functools.partial(cycle_kernel, groups, aux_count),
        name="cycle",
        out_shape=[jax.ShapeDtypeStruct(share, jnp.float32)]
        + [jax.ShapeDtypeStruct(share, jnp.bfloat16)] * (aux_count - 1),
        in_specs=[VMEM] * (1 + groups),
        out_specs=[VMEM] * aux_count,
        scratch_shapes=[pltpu.VMEM((occ_rows * virt, virt), amps.dtype)],
        compiler_params=room(4 * flat.size + 8 * own.size + 8 * padded_rows * virt * virt),
    )(screened, *pieces)

    def spread(value, step):
        perm = [(z, hop_to(z, step, aux_count)) for z in range(aux_count)]
        return lax.ppermute(value, "aux", perm)

    cycle = partials[0]
    for step in range(1, aux_count):
        cycle = cycle + spread(partials[step], step).astype(jnp.float32)

    divided = (cycle / denominator).astype(jnp.bfloat16)

    shares = [divided] + [spread(divided, step) for step in range(1, aux_count)]
    joined = pl.pallas_call(
        functools.partial(join_kernel, aux_count, share_rows),
        name="join",
        out_shape=jax.ShapeDtypeStruct((padded_rows, virt, virt), jnp.bfloat16),
        in_specs=[VMEM] * aux_count,
        compiler_params=room(8 * padded_rows * virt * virt),
    )(*shares)
    return joined[:occ_rows, :, None, :]


def solution(mesh):
    placed = (P("tile", None, None, None), P("aux", None, None), P("aux", None), P(), P(), P())
    return jax.shard_map(
        on_device,
        mesh=mesh,
        in_specs=placed,
        out_specs=P(None, None, "tile", None),
        check_vma=False,
    )
```

```python
import functools

import jax
import jax.numpy as jnp
from jax import lax
from jax.experimental import pallas as pl
from jax.experimental.pallas import tpu as pltpu
from jax.sharding import PartitionSpec as P


def hop_to(i, k, n):
    return i ^ k if n & (n - 1) == 0 else (i + k) % n


def hop_from(i, k, n):
    return i ^ k if n & (n - 1) == 0 else (i + n - k) % n


def ring_to(i, k, n):
    return (i + k) % n


def ring_from(i, k, n):
    return (i + n - k) % n


def load_kernel(owner_hbm, own_hbm, owner_ref, own_ref, sems):
    loads = [
        pltpu.make_async_copy(owner_hbm, owner_ref, sems.at[0]),
        pltpu.make_async_copy(own_hbm, own_ref, sems.at[1]),
    ]
    for load in loads:
        load.start()
    for load in loads:
        load.wait()


def pick(table_ref, index):
    table = table_ref[...]
    places = lax.broadcasted_iota(jnp.int32, table.shape, 1)
    return jnp.sum(jnp.where(places == index, table, jnp.zeros_like(table)))


def pack_kernel(groups, slots_ref, own_ref, mate_ref, *out_refs):
    me = lax.axis_index("tile")
    for step, out_ref in enumerate(out_refs):
        slot = 2 * hop_to(me // 2, step, groups) + me % 2
        column = pick(slots_ref, slot)
        out_ref[0] = own_ref[column]
        out_ref[1] = mate_ref[column]


def denominator_kernel(slots_ref, eps_occ_ref, eps_vir_ref, out_ref):
    share_rows, virt, _ = out_ref.shape
    eps_row = jnp.broadcast_to(eps_vir_ref[...], (virt, virt))
    eps_slot = pick(eps_occ_ref, pick(slots_ref, lax.axis_index("tile")))
    virt_pair = eps_row.T + eps_row - eps_slot
    for row in range(share_rows):
        i = jnp.minimum(lax.axis_index("aux") * share_rows + row, eps_occ_ref.shape[1] - 1)
        out_ref[row] = virt_pair - pick(eps_occ_ref, i)


def cycle_kernel(groups, aux_count, screened_ref, *refs):
    piece_refs, out_refs, amps_ref = refs[:groups], refs[groups:-1], refs[-1]
    me = lax.axis_index("tile")
    occ_rows, virt = screened_ref.shape[1] // amps_ref.shape[1], amps_ref.shape[1]
    for step, piece_ref in enumerate(piece_refs):
        group = hop_from(me // 2, step, groups)
        for part in range(2):
            k = 2 * group + (me + part) % 2
            amps_ref[pl.ds(pl.multiple_of(k * virt, virt), virt), :] = piece_ref[part]
    inter = jnp.dot(
        screened_ref[...], amps_ref[...], preferred_element_type=jnp.float32
    ).astype(jnp.bfloat16)
    share_rows = out_refs[0].shape[0]
    last = (occ_rows - share_rows) * virt
    for step, out_ref in enumerate(out_refs):
        share = hop_to(lax.axis_index("aux"), step, aux_count)
        start = jnp.minimum(share * share_rows * virt, last)
        columns = screened_ref[:, pl.ds(pl.multiple_of(start, virt), share_rows * virt)]
        flipped = lax.dot_general(
            inter, columns, (((0,), (0,)), ((), ())), preferred_element_type=jnp.float32
        )
        for row in range(share_rows):
            out_ref[row] = flipped[:, row * virt : (row + 1) * virt].T.astype(out_ref.dtype)


def join_kernel(aux_count, share_rows, *refs):
    piece_refs, out_ref = refs[:-1], refs[-1]
    me = lax.axis_index("aux")
    for step, piece_ref in enumerate(piece_refs):
        share = ring_from(me, step, aux_count)
        out_ref[pl.ds(share * share_rows, share_rows)] = piece_ref[...]


VMEM = pl.BlockSpec(memory_space=pltpu.VMEM)


def room(bytes_used):
    return pltpu.CompilerParams(vmem_limit_bytes=bytes_used + (1 << 20))


def on_device(amps, fitted, screen, owner, eps_occ, eps_vir):
    virt = amps.shape[-1]
    aux_here, occ_rows, _ = fitted.shape
    tile_count, aux_count = lax.axis_size("tile"), lax.axis_size("aux")
    groups = tile_count // 2
    share_rows = -(-occ_rows // aux_count)
    padded_rows = share_rows * aux_count

    mate = lax.ppermute(amps[0], "tile", [(t, t ^ 1) for t in range(tile_count)])
    slots, own = pl.pallas_call(
        load_kernel,
        name="load",
        out_shape=[
            jax.ShapeDtypeStruct((1, owner.shape[0]), owner.dtype),
            jax.ShapeDtypeStruct(mate.shape, mate.dtype),
        ],
        in_specs=[pl.BlockSpec(memory_space=pl.ANY)] * 2,
        out_specs=[VMEM] * 2,
        scratch_shapes=[pltpu.SemaphoreType.DMA((2,))],
        compiler_params=room(4 * mate.size),
    )(owner[None, :], amps[0])
    mate, slots, own = lax.optimization_barrier((mate, slots, own))
    tile_piece = jax.ShapeDtypeStruct((2, virt, virt), amps.dtype)
    packed = pl.pallas_call(
        functools.partial(pack_kernel, groups),
        name="pack",
        out_shape=[tile_piece] * groups,
        in_specs=[VMEM] * 3,
        out_specs=[VMEM] * groups,
        compiler_params=room(6 * own.size),
    )(slots, own, mate)
    fitted, screen, kept = lax.optimization_barrier((fitted, screen, packed[0]))
    pieces = [kept] + [
        lax.ppermute(
            packed[step],
            "tile",
            [(t, 2 * hop_to(t // 2, step, groups) + t % 2) for t in range(tile_count)],
        )
        for step in range(1, groups)
    ]

    flat = fitted.reshape(aux_here, occ_rows * virt)
    mask = screen.astype(fitted.dtype)
    mask = jnp.repeat(mask, virt, axis=1)
    screened = flat * jnp.repeat(mask, aux_here // screen.shape[0], axis=0)
    share = (share_rows, virt, virt)
    denominator = pl.pallas_call(
        denominator_kernel,
        name="denominator",
        out_shape=jax.ShapeDtypeStruct(share, jnp.float32),
        in_specs=[VMEM] * 3,
        out_specs=VMEM,
        compiler_params=room(8 * share_rows * virt * virt),
    )(slots, eps_occ[None, :], eps_vir[None, :])
    partials = pl.pallas_call(
        functools.partial(cycle_kernel, groups, aux_count),
        name="cycle",
        out_shape=[jax.ShapeDtypeStruct(share, jnp.float32)]
        + [jax.ShapeDtypeStruct(share, jnp.bfloat16)] * (aux_count - 1),
        in_specs=[VMEM] * (1 + groups),
        out_specs=[VMEM] * aux_count,
        scratch_shapes=[pltpu.VMEM((occ_rows * virt, virt), amps.dtype)],
        compiler_params=room(4 * flat.size + 8 * own.size + 8 * padded_rows * virt * virt),
    )(screened, *pieces)

    def spread(value, step, to):
        perm = [(z, to(z, step, aux_count)) for z in range(aux_count)]
        return lax.ppermute(value, "aux", perm)

    cycle = partials[0]
    for step in range(1, aux_count):
        cycle = cycle + spread(partials[step], step, hop_to).astype(jnp.float32)

    divided = (cycle / denominator).astype(jnp.bfloat16)

    shares = [divided] + [spread(divided, step, ring_to) for step in range(1, aux_count)]
    joined = pl.pallas_call(
        functools.partial(join_kernel, aux_count, share_rows),
        name="join",
        out_shape=jax.ShapeDtypeStruct((padded_rows, virt, virt), jnp.bfloat16),
        in_specs=[VMEM] * aux_count,
        compiler_params=room(8 * padded_rows * virt * virt),
    )(*shares)
    return joined[:occ_rows, :, None, :]


def solution(mesh):
    placed = (P("tile", None, None, None), P("aux", None, None), P("aux", None), P(), P(), P())
    return jax.shard_map(
        on_device,
        mesh=mesh,
        in_specs=placed,
        out_specs=P(None, None, "tile", None),
        check_vma=False,
    )
```

```python
import functools

import jax
import jax.numpy as jnp
from jax import lax
from jax.experimental import pallas as pl
from jax.experimental.pallas import tpu as pltpu
from jax.sharding import PartitionSpec as P


def hop_to(i, k, n):
    return i ^ k if n & (n - 1) == 0 else (i + k) % n


def hop_from(i, k, n):
    return i ^ k if n & (n - 1) == 0 else (i + n - k) % n


def ring_to(i, k, n):
    return (i + k) % n


def ring_from(i, k, n):
    return (i + n - k) % n


def load_kernel(owner_hbm, own_hbm, owner_ref, own_ref, sems):
    loads = [
        pltpu.make_async_copy(owner_hbm, owner_ref, sems.at[0]),
        pltpu.make_async_copy(own_hbm, own_ref, sems.at[1]),
    ]
    for load in loads:
        load.start()
    for load in loads:
        load.wait()


def pick(table_ref, index):
    table = table_ref[...]
    places = lax.broadcasted_iota(jnp.int32, table.shape, 1)
    return jnp.sum(jnp.where(places == index, table, jnp.zeros_like(table)))


def pack_kernel(groups, slots_ref, own_ref, mate_ref, *out_refs):
    me = lax.axis_index("tile")
    for step, out_ref in enumerate(out_refs):
        slot = 2 * hop_to(me // 2, step, groups) + me % 2
        column = pick(slots_ref, slot)
        out_ref[me % 2] = own_ref[column]
        out_ref[1 - me % 2] = mate_ref[column]


def denominator_kernel(slots_ref, eps_occ_ref, eps_vir_ref, out_ref):
    share_rows, virt, _ = out_ref.shape
    eps_row = jnp.broadcast_to(eps_vir_ref[...], (virt, virt))
    eps_slot = pick(eps_occ_ref, pick(slots_ref, lax.axis_index("tile")))
    virt_pair = eps_row.T + eps_row - eps_slot
    for row in range(share_rows):
        i = jnp.minimum(lax.axis_index("aux") * share_rows + row, eps_occ_ref.shape[1] - 1)
        out_ref[row] = virt_pair - pick(eps_occ_ref, i)


def inter_term(groups, step, screened_ref, piece_ref):
    pair, virt, _ = piece_ref.shape
    group = hop_from(lax.axis_index("tile") // 2, step, groups)
    start = pl.multiple_of(group * pair * virt, pair * virt)
    columns = screened_ref[:, pl.ds(start, pair * virt)]
    piece = piece_ref[...].reshape(pair * virt, virt)
    return jnp.dot(columns, piece, preferred_element_type=jnp.float32)


def own_kernel(groups, screened_ref, piece_ref, out_ref):
    out_ref[...] = inter_term(groups, 0, screened_ref, piece_ref)


def cycle_share(aux_count, step, inter, screened_ref, out_ref):
    share_rows, virt, _ = out_ref.shape
    share = hop_to(lax.axis_index("aux"), step, aux_count)
    start = jnp.minimum(share * share_rows * virt, screened_ref.shape[1] - share_rows * virt)
    columns = screened_ref[:, pl.ds(pl.multiple_of(start, virt), share_rows * virt)]
    flipped = lax.dot_general(
        inter, columns, (((0,), (0,)), ((), ())), preferred_element_type=jnp.float32
    )
    for row in range(share_rows):
        out_ref[row] = flipped[:, row * virt : (row + 1) * virt].T.astype(out_ref.dtype)


def others_kernel(groups, aux_count, own_ref, screened_ref, *refs):
    piece_refs, inter_ref, out_refs = refs[: groups - 1], refs[groups - 1], refs[groups:]
    total = own_ref[...]
    for step, piece_ref in enumerate(piece_refs, 1):
        total += inter_term(groups, step, screened_ref, piece_ref)
    inter = total.astype(inter_ref.dtype)
    inter_ref[...] = inter
    for step, out_ref in enumerate(out_refs, 1):
        cycle_share(aux_count, step, inter, screened_ref, out_ref)


def kept_kernel(aux_count, inter_ref, screened_ref, out_ref):
    cycle_share(aux_count, 0, inter_ref[...], screened_ref, out_ref)


def join_kernel(aux_count, share_rows, *refs):
    piece_refs, out_ref = refs[:-1], refs[-1]
    me = lax.axis_index("aux")
    for step, piece_ref in enumerate(piece_refs):
        share = ring_from(me, step, aux_count)
        out_ref[pl.ds(share * share_rows, share_rows)] = piece_ref[...]


VMEM = pl.BlockSpec(memory_space=pltpu.VMEM)


def room(bytes_used):
    return pltpu.CompilerParams(vmem_limit_bytes=bytes_used + (1 << 20))


def on_device(amps, fitted, screen, owner, eps_occ, eps_vir):
    virt = amps.shape[-1]
    aux_here, occ_rows, _ = fitted.shape
    tile_count, aux_count = lax.axis_size("tile"), lax.axis_size("aux")
    groups = tile_count // 2
    share_rows = -(-occ_rows // aux_count)
    padded_rows = share_rows * aux_count

    mate = lax.ppermute(amps[0], "tile", [(t, t ^ 1) for t in range(tile_count)])
    slots, own = pl.pallas_call(
        load_kernel,
        name="load",
        out_shape=[
            jax.ShapeDtypeStruct((1, owner.shape[0]), owner.dtype),
            jax.ShapeDtypeStruct(mate.shape, mate.dtype),
        ],
        in_specs=[pl.BlockSpec(memory_space=pl.ANY)] * 2,
        out_specs=[VMEM] * 2,
        scratch_shapes=[pltpu.SemaphoreType.DMA((2,))],
        compiler_params=room(4 * mate.size),
    )(owner[None, :], amps[0])
    mate, slots, own = lax.optimization_barrier((mate, slots, own))
    tile_piece = jax.ShapeDtypeStruct((2, virt, virt), amps.dtype)
    packed = pl.pallas_call(
        functools.partial(pack_kernel, groups),
        name="pack",
        out_shape=[tile_piece] * groups,
        in_specs=[VMEM] * 3,
        out_specs=[VMEM] * groups,
        compiler_params=room(6 * own.size),
    )(slots, own, mate)
    fitted, screen, kept = lax.optimization_barrier((fitted, screen, packed[0]))
    pieces = [kept] + [
        lax.ppermute(
            packed[step],
            "tile",
            [(t, 2 * hop_to(t // 2, step, groups) + t % 2) for t in range(tile_count)],
        )
        for step in range(1, groups)
    ]

    flat = fitted.reshape(aux_here, occ_rows * virt)
    mask = screen.astype(fitted.dtype)
    mask = jnp.repeat(mask, virt, axis=1)
    screened = flat * jnp.repeat(mask, aux_here // screen.shape[0], axis=0)
    share = (share_rows, virt, virt)
    denominator = pl.pallas_call(
        denominator_kernel,
        name="denominator",
        out_shape=jax.ShapeDtypeStruct(share, jnp.float32),
        in_specs=[VMEM] * 3,
        out_specs=VMEM,
        compiler_params=room(8 * share_rows * virt * virt),
    )(slots, eps_occ[None, :], eps_vir[None, :])
    inter_shape = jax.ShapeDtypeStruct((aux_here, virt), jnp.bfloat16)
    grant = room(2 * flat.size + 8 * inter_shape.size + 8 * own.size + 8 * padded_rows * virt * virt)
    inter_own = pl.pallas_call(
        functools.partial(own_kernel, groups),
        name="own",
        out_shape=jax.ShapeDtypeStruct(inter_shape.shape, jnp.float32),
        in_specs=[VMEM] * 2,
        out_specs=VMEM,
        compiler_params=grant,
    )(screened, pieces[0])
    inter, *sent = pl.pallas_call(
        functools.partial(others_kernel, groups, aux_count),
        name="others",
        out_shape=[inter_shape] + [jax.ShapeDtypeStruct(share, jnp.bfloat16)] * (aux_count - 1),
        in_specs=[VMEM] * (1 + groups),
        out_specs=[VMEM] * aux_count,
        compiler_params=grant,
    )(inter_own, screened, *pieces[1:])
    kept_rows = pl.pallas_call(
        functools.partial(kept_kernel, aux_count),
        name="kept",
        out_shape=jax.ShapeDtypeStruct(share, jnp.float32),
        in_specs=[VMEM] * 2,
        out_specs=VMEM,
        compiler_params=grant,
    )(inter, screened)

    def spread(value, step, to):
        perm = [(z, to(z, step, aux_count)) for z in range(aux_count)]
        return lax.ppermute(value, "aux", perm)

    cycle = kept_rows
    for step, partial in enumerate(sent, 1):
        cycle = cycle + spread(partial, step, hop_to).astype(jnp.float32)

    divided = (cycle / denominator).astype(jnp.bfloat16)

    shares = [divided] + [spread(divided, step, ring_to) for step in range(1, aux_count)]
    joined = pl.pallas_call(
        functools.partial(join_kernel, aux_count, share_rows),
        name="join",
        out_shape=jax.ShapeDtypeStruct((padded_rows, virt, virt), jnp.bfloat16),
        in_specs=[VMEM] * aux_count,
        compiler_params=room(8 * padded_rows * virt * virt),
    )(*shares)
    return joined[:occ_rows, :, None, :]


def solution(mesh):
    placed = (P("tile", None, None, None), P("aux", None, None), P("aux", None), P(), P(), P())
    return jax.shard_map(
        on_device,
        mesh=mesh,
        in_specs=placed,
        out_specs=P(None, None, "tile", None),
        check_vma=False,
    )
```
